768 devices in a mesh: wide: 32 (over x_lo, y, core), narrow: 24 (over x_hi, z).
Axes of the slice: x: 4 (x_hi: 2, x_lo: 2; x = x_hi * 2 + x_lo), y: 8, z: 12, core: 2. Of those that a mesh axis runs over, the one named last changes fastest.
Arguments:
- diag_blocks: float32 [32, 512, 512], P('wide'), as said below
- row_panel: bfloat16 [32, 6144, 512], P('wide', 'narrow'), may hold values from -6 to 6
- col_panel: bfloat16 [32, 6144, 512], P('wide', 'narrow'), may hold values from -6 to 6
- row_tiles: int32 [32, 24], P('wide'), may hold values from 0 to 31, as said below
- col_mask: int32 [32, 24], P('wide', 'narrow'), may hold values 0 or 1
- slot_tile: int32 [32], replicated, may hold values from 0 to 31, each once
- trailing: float32 [8192, 6144], P('wide', 'narrow'), may hold values from -6 to 6
Outputs:
- schur_block: float32 [8192, 6144], P('wide', 'narrow')
The draws below stay inside these ranges and needn't reach their ends.
Inputs may be any that keep to these rules, and one draw needn't show every extreme that they name: `row_tiles`: the 24 ids of one supernode are distinct. `slot_tile`: a permutation of the row-tile ids. `diag_blocks`: each block is symmetric and positive definite, its smallest eigenvalue at least 30.
All inputs are finite; a program needn't handle non-finite values. No bound on the sum of `col_mask` on one device may be relied on, other than what follows from the above.
Results may differ from the reference program's by a relative error of at most 0.013.
Values may be sent and summed in bfloat16 or wider, within the bound.
No kernel may reach another device: no remote copies, remote signals or barrier semaphores. Data moves between devices by JAX's collectives and lax.ppermute only.
A program may use at most 64 MiB of HBM per device.

```python
import jax
import jax.numpy as jnp
from jax import lax

SNW = 512
TILE = 256
SN_DEV = 1
NSUP = 32
ROW_TILES = 32
COL_TILES = 24


def draw_diag_blocks(key, part):
    factors = jax.random.normal(key, (NSUP, SNW, SNW), jnp.float32)
    gram = jnp.einsum('sik,sjk->sij', factors, factors, precision=lax.Precision.HIGHEST) / SNW
    gram = 0.5 * (gram + jnp.swapaxes(gram, 1, 2))
    identity = jnp.eye(SNW, dtype=jnp.float32)[None, :, :]
    return (50.0 * (gram + identity)).astype(jnp.float32)


def draw_row_tiles(key, part):
    subkeys = jax.random.split(jax.random.fold_in(key, 11), NSUP)

    def single(subkey):
        return jax.random.permutation(subkey, ROW_TILES)[:COL_TILES].astype(jnp.int32)
    return jax.vmap(single)(subkeys)


def touch_ends(result, own_key, least, high):
    dims = result.shape
    place = [jax.random.randint(jax.random.fold_in(own_key, axis), (), 0, dims[axis]) for axis in range(len(dims))]
    result = result.at[tuple(place)].set(least)
    longest = dims.index(max(dims))
    place[longest] = (place[longest] + 1) % dims[longest]
    return result.at[tuple(place)].set(high)


def level_of(key, extent, shards, smallest, largest):
    gain, own = 1.0, jax.random.fold_in(key, 6)
    for axis_at, blocks in shards:
        draws = jnp.exp(jax.random.uniform(jax.random.fold_in(own, axis_at), (blocks,), jnp.float32, smallest / len(shards), largest / len(shards)))
        gain = gain * jnp.repeat(draws, extent[axis_at] // blocks).reshape([-1 if axis == axis_at else 1 for axis in range(len(extent))])
    return gain


def gaussian(key, shape, spread, most, cuts=(), held_as=jnp.bfloat16):
    values = jax.random.normal(key, shape, jnp.float32) * spread
    if len(cuts) > 0:
        values = level_of(key, shape, cuts, -0.22, 0.18) * values
    return jnp.clip(values, min=-most, max=most).astype(held_as)


def setup_inputs(seed: int = 0) -> dict:
    key_list = jax.random.split(jax.random.key(seed), 8)
    return {
        "diag_blocks": draw_diag_blocks(jax.random.fold_in(key_list[7], 71), 0),
        "row_panel": gaussian(key_list[1], (NSUP, COL_TILES * TILE, SNW), 1.0, 6.0, ((0, 32), (1, 24))),
        "col_panel": gaussian(key_list[2], (NSUP, COL_TILES * TILE, SNW), 1.0, 6.0, ((0, 32), (1, 24))),
        "row_tiles": draw_row_tiles(jax.random.fold_in(key_list[7], 71), 0),
        "col_mask": touch_ends((jax.random.randint(key_list[4], (NSUP, COL_TILES), 0, 2) < 1).astype(jnp.int32), jax.random.fold_in(key_list[4], 1), 0, 1),
        "slot_tile": jax.random.permutation(key_list[5], ROW_TILES).astype(jnp.int32),
        "trailing": gaussian(key_list[6], (ROW_TILES * TILE, COL_TILES * TILE), 1.0, 6.0, ((0, 32), (1, 24)), jnp.float32),
    }


def solve_rows(panel, factor_low):
    solved = lax.linalg.triangular_solve(factor_low, panel.astype(jnp.float32), left_side=False, lower=True, transpose_a=True)
    return solved.astype(jnp.bfloat16)

def member(diagonal, rows_in, cols_in, tile_ids, present, slot_of):
    factor_low = jnp.linalg.cholesky(diagonal)
    left_side = solve_rows(rows_in, factor_low).astype(jnp.float32)
    right_side = solve_rows(cols_in, factor_low).astype(jnp.float32)
    right_side = right_side * jnp.repeat(present.astype(jnp.float32), TILE)[:, None]
    products = jnp.dot(left_side, right_side.T, precision=lax.Precision.HIGHEST)
    blocks = products.reshape(COL_TILES, TILE, COL_TILES * TILE)
    placed = jnp.zeros((ROW_TILES, TILE, COL_TILES * TILE), jnp.float32)
    return placed.at[slot_of[tile_ids]].add(blocks)

def reference(diag_blocks, row_panel, col_panel, row_tiles, col_mask, slot_tile, trailing):
    positions = jnp.arange(ROW_TILES, dtype=jnp.int32)
    slot_of = jnp.zeros((ROW_TILES,), jnp.int32).at[slot_tile].set(positions)
    groups = (diag_blocks.reshape(ROW_TILES, SN_DEV, SNW, SNW), row_panel.reshape(ROW_TILES, SN_DEV, COL_TILES * TILE, SNW), col_panel.reshape(ROW_TILES, SN_DEV, COL_TILES * TILE, SNW), row_tiles.reshape(ROW_TILES, SN_DEV, COL_TILES), col_mask.reshape(ROW_TILES, SN_DEV, COL_TILES))

    def group_step(running, inputs):
        diagonal, rows_in, cols_in, tile_ids, present = inputs
        partial_value = jnp.zeros((ROW_TILES, TILE, COL_TILES * TILE), jnp.float32)
        for which in range(SN_DEV):
            partial_value = partial_value + member(diagonal[which], rows_in[which], cols_in[which], tile_ids[which], present[which], slot_of)
        rounded = lax.optimization_barrier(partial_value.astype(jnp.bfloat16))
        return (running + rounded.astype(jnp.float32), None)
    start_sum = jnp.zeros((ROW_TILES, TILE, COL_TILES * TILE), jnp.float32)
    update, _ = lax.scan(group_step, start_sum, groups)
    return trailing - update.reshape(ROW_TILES * TILE, COL_TILES * TILE)
```

```python
import jax
import jax.numpy as jnp
from jax import lax
from jax.experimental import pallas as pl
from jax.experimental.pallas import tpu as pltpu
from jax.sharding import Mesh, PartitionSpec as P

BLOCK = 128
GROUP = 8

def invert_block(block):
    size = block.shape[0]
    lanes = lax.broadcasted_iota(jnp.int32, (1, size), 1)
    for j in range(0, size, GROUP):
        columns = [
            jnp.broadcast_to(block[:, j + k : j + k + 1], (size, size)) for k in range(GROUP)
        ]
        pivots = [
            [columns[b][j + a : j + a + 1, :] if b >= a else None for b in range(GROUP)]
            for a in range(GROUP)
        ]
        rows = []
        for a in range(GROUP):
            inside = (lanes >= j) & (lanes < j + GROUP)
            unit = jnp.where(lanes == j + a, 1.0, 0.0)
            rows.append(jnp.where(inside, unit, block[j + a : j + a + 1, :]))
        factors = [None] * GROUP
        for k in range(GROUP):
            scale = 1.0 / pivots[k][k]
            factors[k] = {}
            for a in range(k + 1, GROUP):
                factor = pivots[k][a] * scale
                factors[k][a] = factor
                rows[a] = rows[a] - factor * rows[k]
                for b in range(a, GROUP):
                    pivots[a][b] = pivots[a][b] - factor * pivots[k][b]
            pivots[k][k] = scale
        for k in reversed(range(GROUP)):
            solved = rows[k] * pivots[k][k]
            for a in range(k + 1, GROUP):
                solved = solved - factors[k][a] * rows[a]
            rows[k] = solved
        outside = (lanes < j) | (lanes >= j + GROUP)
        rest = jnp.where(outside, block, 0.0)
        for k in range(GROUP):
            rest = rest - columns[k] * rows[k]
        parts = []
        if j > 0:
            parts.append(rest[:j])
        parts.append(jnp.concatenate(rows, axis=0))
        if j + GROUP < size:
            parts.append(rest[j + GROUP :])
        block = jnp.concatenate(parts, axis=0)
    return block


def exact_dot(left, right):
    return jnp.dot(left, right, precision=lax.Precision.HIGHEST, preferred_element_type=jnp.float32)


def solve_kernel(diag_ref, panel_ref, out_ref, work_ref, rhs_ref):
    width = diag_ref.shape[0]
    tile = panel_ref.shape[0]
    work_ref[...] = diag_ref[...]
    rhs_ref[...] = panel_ref[...].astype(jnp.float32).T
    steps = width // BLOCK
    for k in range(steps):
        here = slice(k * BLOCK, (k + 1) * BLOCK)
        inverse = invert_block(work_ref[here, here])
        solved = exact_dot(inverse, rhs_ref[here, :])
        rhs_ref[here, :] = solved
        last = (k + 1) * BLOCK
        if last < width:
            rest = exact_dot(inverse, work_ref[here, last:])
            work_ref[here, last:] = rest
        for i in range(steps):
            if i == k:
                continue
            there = slice(i * BLOCK, (i + 1) * BLOCK)
            multiplier = work_ref[there, here]
            rhs_ref[there, :] = rhs_ref[there, :] - exact_dot(multiplier, solved)
            if last < width:
                work_ref[there, last:] = work_ref[there, last:] - exact_dot(multiplier, rest)
    solved = rhs_ref[...]
    high = solved.astype(jnp.bfloat16)
    low = (solved - high.astype(jnp.float32)).astype(jnp.bfloat16)
    out_ref[:, :tile] = high
    out_ref[:, tile:] = low


def solve_panel(diag, panel):
    width, tile = diag.shape[0], panel.shape[0]
    return pl.pallas_call(
        solve_kernel,
        out_shape=jax.ShapeDtypeStruct((width, 2 * tile), jnp.bfloat16),
        scratch_shapes=[
            pltpu.VMEM((width, width), jnp.float32),
            pltpu.VMEM((width, tile), jnp.float32),
        ],
        name="solve_panel",
    )(diag, panel)


def product_kernel(table_ref, tile_ref, solved_ref, *rest):
    out_ref = rest[-1]
    step = pl.program_id(0)
    present = table_ref[step] >= 0
    width = out_ref.shape[1]

    @pl.when(present)
    def _():
        both = jnp.dot(tile_ref[...], solved_ref[...], preferred_element_type=jnp.float32)
        value = both[:, :width] + both[:, width:]
        if len(rest) == 2:
            value = value + rest[0][...].astype(jnp.float32)
        out_ref[...] = value.astype(out_ref.dtype)

    @pl.when(jnp.logical_not(present))
    def _():
        if len(rest) == 2:
            out_ref[...] = rest[0][...]
        else:
            out_ref[...] = jnp.zeros_like(out_ref)


def placed_products(table, tiles, solved, received, name):
    slots, width = table.shape[0], tiles.shape[1]
    tile = solved.shape[1] // 2
    by_slot = pl.BlockSpec((tile, tile), lambda i, table: (i, 0))
    in_specs = [
        pl.BlockSpec((tile, width), lambda i, table: (jnp.maximum(table[i], 0), 0)),
        pl.BlockSpec((width, 2 * tile), lambda i, table: (0, 0)),
    ]
    operands = [table, tiles, solved]
    if received is not None:
        in_specs.append(by_slot)
        operands.append(received)
    return pl.pallas_call(
        product_kernel,
        grid_spec=pltpu.PrefetchScalarGridSpec(
            num_scalar_prefetch=1, grid=(slots,), in_specs=in_specs, out_specs=by_slot
        ),
        out_shape=jax.ShapeDtypeStruct((slots * tile, tile), jnp.bfloat16),
        name=name,
    )(*operands)


def local(diag_blocks, row_panel, col_panel, row_tiles, col_mask, slot_tile, trailing):
    tile = trailing.shape[0]
    pair = lax.all_gather(row_panel[0], "x_hi", axis=0, tiled=True)
    tiles = lax.all_gather(pair, "z", axis=0, tiled=True)
    solved = solve_panel(diag_blocks[0], col_panel[0])

    count = row_tiles.shape[1]
    halves = lax.axis_size("x_hi")
    order = jnp.arange(count, dtype=jnp.int32)
    place = (order % (count // halves)) * halves + order // (count // halves)
    match = slot_tile[:, None] == row_tiles[0][None, :]
    table = jnp.max(jnp.where(match & (col_mask[0, 0] != 0), place[None, :], -1), axis=1)
    table = table.reshape(-1, 2)
    core = lax.axis_index("core")
    mine = jnp.where(core == 0, table[:, 0], table[:, 1])
    other = jnp.where(core == 0, table[:, 1], table[:, 0])

    sent = placed_products(other, tiles, solved, None, "products_sent")
    received = lax.ppermute(sent, "core", [(0, 1), (1, 0)])
    partial = placed_products(mine, tiles, solved, received, "products_kept")
    pieces = lax.all_to_all(partial, ("x_lo", "y"), 0, 0, tiled=True)
    pieces = pieces.reshape(-1, tile, tile).astype(jnp.float32)
    return trailing - jnp.sum(pieces, axis=0)


def solution(mesh):
    wide, narrow = mesh.shape["wide"], mesh.shape["narrow"]
    split = Mesh(
        mesh.devices.reshape(2, wide // 4, 2, 2, narrow // 2), ("x_lo", "y", "core", "x_hi", "z")
    )
    w, n = ("x_lo", "y", "core"), ("x_hi", "z")
    placed = (P(w), P(w, n), P(w, n), P(w), P(w, n), P(), P(w, n))
    return jax.shard_map(local, mesh=split, in_specs=placed, out_specs=P(w, n), check_vma=False)
```

```python
import jax
import jax.numpy as jnp
from jax import lax
from jax.experimental import pallas as pl
from jax.experimental.pallas import tpu as pltpu
from jax.sharding import Mesh, PartitionSpec as P


BLOCK = 128
GROUP = 8
FIRST_ROWS = 160


def invert_block(block):
    size = block.shape[0]
    lanes = lax.broadcasted_iota(jnp.int32, (1, size), 1)
    for j in range(0, size, GROUP):
        columns = [
            jnp.broadcast_to(block[:, j + k : j + k + 1], (size, size)) for k in range(GROUP)
        ]
        pivots = [
            [columns[b][j + a : j + a + 1, :] if b >= a else None for b in range(GROUP)]
            for a in range(GROUP)
        ]
        rows = []
        for a in range(GROUP):
            inside = (lanes >= j) & (lanes < j + GROUP)
            unit = jnp.where(lanes == j + a, 1.0, 0.0)
            rows.append(jnp.where(inside, unit, block[j + a : j + a + 1, :]))
        factors = [None] * GROUP
        for k in range(GROUP):
            scale = 1.0 / pivots[k][k]
            factors[k] = {}
            for a in range(k + 1, GROUP):
                factor = pivots[k][a] * scale
                factors[k][a] = factor
                rows[a] = rows[a] - factor * rows[k]
                for b in range(a, GROUP):
                    pivots[a][b] = pivots[a][b] - factor * pivots[k][b]
            pivots[k][k] = scale
        for k in reversed(range(GROUP)):
            solved = rows[k] * pivots[k][k]
            for a in range(k + 1, GROUP):
                solved = solved - factors[k][a] * rows[a]
            rows[k] = solved
        outside = (lanes < j) | (lanes >= j + GROUP)
        rest = jnp.where(outside, block, 0.0)
        for k in range(GROUP):
            rest = rest - columns[k] * rows[k]
        parts = []
        if j > 0:
            parts.append(rest[:j])
        parts.append(jnp.concatenate(rows, axis=0))
        if j + GROUP < size:
            parts.append(rest[j + GROUP :])
        block = jnp.concatenate(parts, axis=0)
    return block


def exact_dot(left, right):
    return jnp.dot(left, right, precision=lax.Precision.HIGHEST, preferred_element_type=jnp.float32)


def solve_kernel(diag_ref, panel_ref, out_ref, work_ref, rhs_ref):
    width = diag_ref.shape[0]
    tile = panel_ref.shape[0]
    work_ref[...] = diag_ref[...]
    rhs_ref[...] = panel_ref[...].astype(jnp.float32).T
    steps = width // BLOCK
    for k in range(steps):
        here = slice(k * BLOCK, (k + 1) * BLOCK)
        inverse = invert_block(work_ref[here, here])
        solved = exact_dot(inverse, rhs_ref[here, :])
        rhs_ref[here, :] = solved
        last = (k + 1) * BLOCK
        if last < width:
            rest = exact_dot(inverse, work_ref[here, last:])
            work_ref[here, last:] = rest
        for i in range(steps):
            if i == k:
                continue
            there = slice(i * BLOCK, (i + 1) * BLOCK)
            multiplier = work_ref[there, here]
            rhs_ref[there, :] = rhs_ref[there, :] - exact_dot(multiplier, solved)
            if last < width:
                work_ref[there, last:] = work_ref[there, last:] - exact_dot(multiplier, rest)
    solved = rhs_ref[...]
    high = solved.astype(jnp.bfloat16)
    low = (solved - high.astype(jnp.float32)).astype(jnp.bfloat16)
    out_ref[:, :tile] = high
    out_ref[:, tile:] = low


def solve_panel(diag, panel):
    width, tile = diag.shape[0], panel.shape[0]
    return pl.pallas_call(
        solve_kernel,
        out_shape=jax.ShapeDtypeStruct((width, 2 * tile), jnp.bfloat16),
        scratch_shapes=[
            pltpu.VMEM((width, width), jnp.float32),
            pltpu.VMEM((width, tile), jnp.float32),
        ],
        name="solve_panel",
    )(diag, panel)


def product_kernel(table_ref, tiles_ref, solved_ref, sent_ref, kept_ref):
    slots, _, width = sent_ref.shape
    solved = solved_ref[...]

    def place(slot, out_ref, row):
        index = table_ref[row, slot]

        @pl.when(index >= 0)
        def _():
            both = jnp.dot(tiles_ref[index], solved, preferred_element_type=jnp.float32)
            out_ref[slot] = (both[:, :width] + both[:, width:]).astype(out_ref.dtype)

        @pl.when(index < 0)
        def _():
            out_ref[slot] = jnp.zeros(out_ref.shape[1:], out_ref.dtype)

    def step(slot, carry):
        place(slot, sent_ref, 0)
        place(slot, kept_ref, 1)
        return carry

    lax.fori_loop(0, slots, step, 0)


def placed_products(table, tiles, solved):
    half = jax.ShapeDtypeStruct(
        (table.shape[1], tiles.shape[1], solved.shape[1] // 2), jnp.bfloat16
    )
    whole = pl.BlockSpec(memory_space=pltpu.VMEM)
    return pl.pallas_call(
        product_kernel,
        in_specs=[pl.BlockSpec(memory_space=pltpu.SMEM), whole, whole],
        out_specs=[whole, whole],
        out_shape=[half, half],
    )(table, tiles, solved)


def local(diag_blocks, row_panel, col_panel, row_tiles, col_mask, slot_tile, trailing):
    width = row_panel.shape[2]
    count = row_tiles.shape[1]
    halves = lax.axis_size("x_hi")

    first, second = row_panel[0, :FIRST_ROWS], row_panel[0, FIRST_ROWS:]
    first = lax.all_gather(first, "x_hi", axis=0, tiled=True)
    first, second = lax.optimization_barrier((first, second))
    second = lax.all_gather(second, "x_hi", axis=0, tiled=True)
    solved = solve_panel(diag_blocks[0], col_panel[0])
    second, solved = lax.optimization_barrier((second, solved))
    gathered = []
    for pair in (first, second):
        rows = lax.all_gather(pair, "z", axis=0, tiled=True)
        gathered.append(rows.reshape(count, pair.shape[0] // halves, width))

    order = jnp.arange(count, dtype=jnp.int32)
    place = (order % (count // halves)) * halves + order // (count // halves)
    match = slot_tile[:, None] == row_tiles[0][None, :]
    table = jnp.max(jnp.where(match & (col_mask[0, 0] != 0), place[None, :], -1), axis=1)
    table = table.reshape(-1, 2).T
    core = lax.axis_index("core")
    table = jnp.where(core == 0, table[::-1], table)

    stripes = []
    for rows in gathered:
        sent, kept = placed_products(table, rows, solved)
        received = lax.ppermute(sent, "core", [(0, 1), (1, 0)])
        partial = kept.astype(jnp.float32) + received.astype(jnp.float32)
        partial = partial.astype(jnp.bfloat16)
        if stripes:
            partial, stripes[-1] = lax.optimization_barrier((partial, stripes[-1]))
        pieces = lax.all_to_all(partial, ("x_lo", "y"), 0, 0, tiled=True)
        stripes.append(jnp.sum(pieces.astype(jnp.float32), axis=0))
    return trailing - jnp.concatenate(stripes, axis=0)


def solution(mesh):
    wide, narrow = mesh.shape["wide"], mesh.shape["narrow"]
    split = Mesh(
        mesh.devices.reshape(2, wide // 4, 2, 2, narrow // 2), ("x_lo", "y", "core", "x_hi", "z")
    )
    w, n = ("x_lo", "y", "core"), ("x_hi", "z")
    placed = (P(w), P(w, n), P(w, n), P(w), P(w, n), P(), P(w, n))

    return jax.shard_map(local, mesh=split, in_specs=placed, out_specs=P(w, n), check_vma=False)
```

```python
import jax
import jax.numpy as jnp
from jax import lax
from jax.experimental import pallas as pl
from jax.experimental.pallas import tpu as pltpu
from jax.sharding import Mesh, PartitionSpec as P


BLOCK = 128
GROUP = 8
FIRST_ROWS = 192
TILES_PER_STEP = 6


def invert_block(block):
    size = block.shape[0]
    lanes = lax.broadcasted_iota(jnp.int32, (1, size), 1)
    for j in range(0, size, GROUP):
        columns = [
            jnp.broadcast_to(block[:, j + k : j + k + 1], (size, size)) for k in range(GROUP)
        ]
        pivots = [
            [columns[b][j + a : j + a + 1, :] if b >= a else None for b in range(GROUP)]
            for a in range(GROUP)
        ]
        rows = []
        for a in range(GROUP):
            inside = (lanes >= j) & (lanes < j + GROUP)
            unit = jnp.where(lanes == j + a, 1.0, 0.0)
            rows.append(jnp.where(inside, unit, block[j + a : j + a + 1, :]))
        factors = [None] * GROUP
        for k in range(GROUP):
            scale = 1.0 / pivots[k][k]
            factors[k] = {}
            for a in range(k + 1, GROUP):
                factor = pivots[k][a] * scale
                factors[k][a] = factor
                rows[a] = rows[a] - factor * rows[k]
                for b in range(a, GROUP):
                    pivots[a][b] = pivots[a][b] - factor * pivots[k][b]
            pivots[k][k] = scale
        for k in reversed(range(GROUP)):
            solved = rows[k] * pivots[k][k]
            for a in range(k + 1, GROUP):
                solved = solved - factors[k][a] * rows[a]
            rows[k] = solved
        outside = (lanes < j) | (lanes >= j + GROUP)
        rest = jnp.where(outside, block, 0.0)
        for k in range(GROUP):
            rest = rest - columns[k] * rows[k]
        parts = []
        if j > 0:
            parts.append(rest[:j])
        parts.append(jnp.concatenate(rows, axis=0))
        if j + GROUP < size:
            parts.append(rest[j + GROUP :])
        block = jnp.concatenate(parts, axis=0)
    return block


def exact_dot(left, right):
    return jnp.dot(left, right, precision=lax.Precision.HIGHEST, preferred_element_type=jnp.float32)


def solve_kernel(diag_ref, panel_ref, out_ref, work_ref, rhs_ref):
    width = diag_ref.shape[0]
    tile = panel_ref.shape[0]
    work_ref[...] = diag_ref[...]
    rhs_ref[...] = panel_ref[...].astype(jnp.float32).T
    steps = width // BLOCK
    for k in range(steps):
        here = slice(k * BLOCK, (k + 1) * BLOCK)
        inverse = invert_block(work_ref[here, here])
        solved = exact_dot(inverse, rhs_ref[here, :])
        rhs_ref[here, :] = solved
        last = (k + 1) * BLOCK
        if last < width:
            rest = exact_dot(inverse, work_ref[here, last:])
            work_ref[here, last:] = rest
        for i in range(steps):
            if i == k:
                continue
            there = slice(i * BLOCK, (i + 1) * BLOCK)
            multiplier = work_ref[there, here]
            rhs_ref[there, :] = rhs_ref[there, :] - exact_dot(multiplier, solved)
            if last < width:
                work_ref[there, last:] = work_ref[there, last:] - exact_dot(multiplier, rest)
    solved = rhs_ref[...]
    high = solved.astype(jnp.bfloat16)
    low = (solved - high.astype(jnp.float32)).astype(jnp.bfloat16)
    out_ref[:, :tile] = high
    out_ref[:, tile:] = low


def solve_panel(diag, panel):
    width, tile = diag.shape[0], panel.shape[0]
    return pl.pallas_call(
        solve_kernel,
        out_shape=jax.ShapeDtypeStruct((width, 2 * tile), jnp.bfloat16),
        scratch_shapes=[
            pltpu.VMEM((width, width), jnp.float32),
            pltpu.VMEM((width, tile), jnp.float32),
        ],
        name="solve_panel",
    )(diag, panel)


def product_kernel(dest_ref, tiles_ref, solved_ref, sent_ref, kept_ref):
    slots, rows, width = sent_ref.shape
    tiles = tiles_ref.shape[0]
    step = pl.program_id(0)

    @pl.when(step == 0)
    def _():
        sent_ref[...] = jnp.zeros(sent_ref.shape, sent_ref.dtype)
        kept_ref[...] = jnp.zeros(kept_ref.shape, kept_ref.dtype)

    stacked = tiles_ref[...].reshape(tiles * rows, tiles_ref.shape[2])
    both = jnp.dot(stacked, solved_ref[...], preferred_element_type=jnp.float32)
    value = (both[:, :width] + both[:, width:]).astype(sent_ref.dtype)
    for t in range(tiles):
        dest = dest_ref[step * tiles + t]
        part = value[t * rows : (t + 1) * rows]

        @pl.when((dest >= 0) & (dest < slots))
        def _():
            sent_ref[dest] = part

        @pl.when(dest >= slots)
        def _():
            kept_ref[dest - slots] = part


def placed_products(dest, tiles, solved, slots):
    count, rows, width = tiles.shape
    tile = solved.shape[1] // 2
    half = jax.ShapeDtypeStruct((slots, rows, tile), jnp.bfloat16)
    out = pl.BlockSpec((slots, rows, tile), lambda i, dest: (0, 0, 0))
    return pl.pallas_call(
        product_kernel,
        grid_spec=pltpu.PrefetchScalarGridSpec(
            num_scalar_prefetch=1,
            grid=(count // TILES_PER_STEP,),
            in_specs=[
                pl.BlockSpec((TILES_PER_STEP, rows, width), lambda i, dest: (i, 0, 0)),
                pl.BlockSpec((width, 2 * tile), lambda i, dest: (0, 0)),
            ],
            out_specs=[out, out],
        ),
        out_shape=[half, half],
    )(dest, tiles, solved)


def local(diag_blocks, row_panel, col_panel, row_tiles, col_mask, slot_tile, trailing):
    width = row_panel.shape[2]
    count = row_tiles.shape[1]
    halves = lax.axis_size("x_hi")

    first = lax.all_gather(row_panel[0, :FIRST_ROWS], "x_hi", axis=0, tiled=True)
    first, rest = lax.optimization_barrier((first, row_panel))
    second = lax.all_gather(rest[0, FIRST_ROWS:], "x_hi", axis=0, tiled=True)
    solved = solve_panel(diag_blocks[0], col_panel[0])
    second, solved = lax.optimization_barrier((second, solved))
    gathered = []
    for pair in (first, second):
        rows = lax.all_gather(pair, "z", axis=0, tiled=True)
        gathered.append(rows.reshape(count, pair.shape[0] // halves, width))

    slots = slot_tile.shape[0] // 2
    ids = row_tiles[0].reshape(halves, count // halves).T.reshape(count)
    positions = jnp.arange(2 * slots, dtype=jnp.int32)
    match = slot_tile[None, :] == ids[:, None]
    kept_here = (positions % 2 == lax.axis_index("core")).astype(jnp.int32)
    target = jnp.where(col_mask[0, 0] != 0, positions // 2 + slots * kept_here, -1)
    dest = jnp.max(jnp.where(match, target[None, :], -1), axis=1)

    stripes = []
    for rows in gathered:
        sent, kept = placed_products(dest, rows, solved, slots)
        received = lax.ppermute(sent, "core", [(0, 1), (1, 0)])
        partial = kept.astype(jnp.float32) + received.astype(jnp.float32)
        partial = partial.astype(jnp.bfloat16)
        if stripes:
            partial, stripes[-1] = lax.optimization_barrier((partial, stripes[-1]))
        pieces = lax.all_to_all(partial, ("x_lo", "y"), 0, 0, tiled=True)
        stripes.append(jnp.sum(pieces.astype(jnp.float32), axis=0))
    return trailing - jnp.concatenate(stripes, axis=0)


def solution(mesh):
    wide, narrow = mesh.shape["wide"], mesh.shape["narrow"]
    split = Mesh(
        mesh.devices.reshape(2, wide // 4, 2, 2, narrow // 2), ("x_lo", "y", "core", "x_hi", "z")
    )
    w, n = ("x_lo", "y", "core"), ("x_hi", "z")
    placed = (P(w), P(w, n), P(w, n), P(w), P(w, n), P(), P(w, n))

    return jax.shard_map(local, mesh=split, in_specs=placed, out_specs=P(w, n), check_vma=False)
```

```python
import jax
import jax.numpy as jnp
from jax import lax
from jax.experimental import pallas as pl
from jax.experimental.pallas import tpu as pltpu
from jax.sharding import Mesh, PartitionSpec as P


BLOCK = 128
GROUP = 8
FIRST_ROWS = 128
SYNC_ROWS = 32
TILES_PER_STEP = 6


def invert_block(block):
    size = block.shape[0]
    lanes = lax.broadcasted_iota(jnp.int32, (1, size), 1)
    for j in range(0, size, GROUP):
        columns = [
            jnp.broadcast_to(block[:, j + k : j + k + 1], (size, size)) for k in range(GROUP)
        ]
        pivots = [
            [columns[b][j + a : j + a + 1, :] if b >= a else None for b in range(GROUP)]
            for a in range(GROUP)
        ]
        rows = []
        for a in range(GROUP):
            inside = (lanes >= j) & (lanes < j + GROUP)
            unit = jnp.where(lanes == j + a, 1.0, 0.0)
            rows.append(jnp.where(inside, unit, block[j + a : j + a + 1, :]))
        factors = [None] * GROUP
        for k in range(GROUP):
            scale = 1.0 / pivots[k][k]
            factors[k] = {}
            for a in range(k + 1, GROUP):
                factor = pivots[k][a] * scale
                factors[k][a] = factor
                rows[a] = rows[a] - factor * rows[k]
                for b in range(a, GROUP):
                    pivots[a][b] = pivots[a][b] - factor * pivots[k][b]
            pivots[k][k] = scale
        for k in reversed(range(GROUP)):
            solved = rows[k] * pivots[k][k]
            for a in range(k + 1, GROUP):
                solved = solved - factors[k][a] * rows[a]
            rows[k] = solved
        outside = (lanes < j) | (lanes >= j + GROUP)
        rest = jnp.where(outside, block, 0.0)
        for k in range(GROUP):
            rest = rest - columns[k] * rows[k]
        parts = []
        if j > 0:
            parts.append(rest[:j])
        parts.append(jnp.concatenate(rows, axis=0))
        if j + GROUP < size:
            parts.append(rest[j + GROUP :])
        block = jnp.concatenate(parts, axis=0)
    return block


def exact_dot(left, right):
    return jnp.dot(left, right, precision=lax.Precision.HIGHEST, preferred_element_type=jnp.float32)


def solve_kernel(diag_ref, panel_ref, out_ref, work_ref, rhs_ref):
    width = diag_ref.shape[0]
    tile = panel_ref.shape[0]
    work_ref[...] = diag_ref[...]
    rhs_ref[...] = panel_ref[...].astype(jnp.float32).T
    steps = width // BLOCK
    for k in range(steps):
        here = slice(k * BLOCK, (k + 1) * BLOCK)
        inverse = invert_block(work_ref[here, here])
        solved = exact_dot(inverse, rhs_ref[here, :])
        rhs_ref[here, :] = solved
        last = (k + 1) * BLOCK
        if last < width:
            rest = exact_dot(inverse, work_ref[here, last:])
            work_ref[here, last:] = rest
        for i in range(steps):
            if i == k:
                continue
            there = slice(i * BLOCK, (i + 1) * BLOCK)
            multiplier = work_ref[there, here]
            rhs_ref[there, :] = rhs_ref[there, :] - exact_dot(multiplier, solved)
            if last < width:
                work_ref[there, last:] = work_ref[there, last:] - exact_dot(multiplier, rest)
    solved = rhs_ref[...]
    high = solved.astype(jnp.bfloat16)
    low = (solved - high.astype(jnp.float32)).astype(jnp.bfloat16)
    out_ref[:, :tile] = high
    out_ref[:, tile:] = low


def solve_panel(diag, panel):
    width, tile = diag.shape[0], panel.shape[0]
    return pl.pallas_call(
        solve_kernel,
        out_shape=jax.ShapeDtypeStruct((width, 2 * tile), jnp.bfloat16),
        scratch_shapes=[
            pltpu.VMEM((width, width), jnp.float32),
            pltpu.VMEM((width, tile), jnp.float32),
        ],
        name="solve_panel",
    )(diag, panel)


def product_kernel(dest_ref, *refs):
    *tile_refs, solved_ref, sent_ref, kept_ref = refs
    slots, _, width = sent_ref.shape
    step = pl.program_id(0)

    @pl.when(step == 0)
    def _():
        sent_ref[...] = jnp.zeros(sent_ref.shape, sent_ref.dtype)
        kept_ref[...] = jnp.zeros(kept_ref.shape, kept_ref.dtype)

    low = 0
    for tiles_ref in tile_refs:
        tiles, rows, depth = tiles_ref.shape
        stacked = tiles_ref[...].reshape(tiles * rows, depth)
        both = jnp.dot(stacked, solved_ref[...], preferred_element_type=jnp.float32)
        value = (both[:, :width] + both[:, width:]).astype(sent_ref.dtype)
        high = low + rows
        for t in range(tiles):
            dest = dest_ref[step * tiles + t]
            part = value[t * rows : (t + 1) * rows]

            @pl.when((dest >= 0) & (dest < slots))
            def _():
                sent_ref[dest, low:high] = part

            @pl.when(dest >= slots)
            def _():
                kept_ref[dest - slots, low:high] = part

        low = high


def placed_products(dest, groups, solved, slots):
    count, _, width = groups[0].shape
    rows = sum(group.shape[1] for group in groups)
    tile = solved.shape[1] // 2
    half = jax.ShapeDtypeStruct((slots, rows, tile), jnp.bfloat16)
    out = pl.BlockSpec((slots, rows, tile), lambda i, dest: (0, 0, 0))
    in_specs = [
        pl.BlockSpec((TILES_PER_STEP, group.shape[1], width), lambda i, dest: (i, 0, 0))
        for group in groups
    ]
    in_specs.append(pl.BlockSpec((width, 2 * tile), lambda i, dest: (0, 0)))
    return pl.pallas_call(
        product_kernel,
        grid_spec=pltpu.PrefetchScalarGridSpec(
            num_scalar_prefetch=1,
            grid=(count // TILES_PER_STEP,),
            in_specs=in_specs,
            out_specs=[out, out],
        ),
        out_shape=[half, half],
    )(dest, *groups, solved)


def local(diag_blocks, row_panel, col_panel, row_tiles, col_mask, slot_tile, trailing):
    width = row_panel.shape[2]
    count = row_tiles.shape[1]
    halves = lax.axis_size("x_hi")

    def over_x(rows):
        return lax.all_gather(rows, "x_hi", axis=0)

    def over_z(pair):
        rows = lax.all_gather(pair.reshape(-1, width), "z", axis=0, tiled=True)
        return rows.reshape(count, pair.shape[1], width)

    first = over_x(row_panel[0, :FIRST_ROWS])
    first, rest = lax.optimization_barrier((first, row_panel))
    rest = over_x(rest[0, FIRST_ROWS:])
    early = over_z(first)
    middle, late = rest[:, :SYNC_ROWS], over_z(rest[:, SYNC_ROWS:])
    solved = solve_panel(diag_blocks[0], col_panel[0])
    middle, solved = lax.optimization_barrier((middle, solved))
    gathered = ((early, over_z(middle)), (late,))

    slots = slot_tile.shape[0] // 2
    ids = row_tiles[0].reshape(halves, count // halves).T.reshape(count)
    positions = jnp.arange(2 * slots, dtype=jnp.int32)
    match = slot_tile[None, :] == ids[:, None]
    kept_here = (positions % 2 == lax.axis_index("core")).astype(jnp.int32)
    target = jnp.where(col_mask[0, 0] != 0, positions // 2 + slots * kept_here, -1)
    dest = jnp.max(jnp.where(match, target[None, :], -1), axis=1)

    stripes = []
    for groups in gathered:
        sent, kept = placed_products(dest, groups, solved, slots)
        received = lax.ppermute(sent, "core", [(0, 1), (1, 0)])
        partial = kept.astype(jnp.float32) + received.astype(jnp.float32)
        partial = partial.astype(jnp.bfloat16)
        if stripes:
            partial, stripes[-1] = lax.optimization_barrier((partial, stripes[-1]))
        pieces = lax.all_to_all(partial, ("x_lo", "y"), 0, 0, tiled=True)
        stripes.append(jnp.sum(pieces.astype(jnp.float32), axis=0))
    return trailing - jnp.concatenate(stripes, axis=0)


def solution(mesh):
    wide, narrow = mesh.shape["wide"], mesh.shape["narrow"]
    split = Mesh(
        mesh.devices.reshape(2, wide // 4, 2, 2, narrow // 2), ("x_lo", "y", "core", "x_hi", "z")
    )
    w, n = ("x_lo", "y", "core"), ("x_hi", "z")
    placed = (P(w), P(w, n), P(w, n), P(w), P(w, n), P(), P(w, n))

    return jax.shard_map(local, mesh=split, in_specs=placed, out_specs=P(w, n), check_vma=False)
```

```python
import jax
import jax.numpy as jnp
from jax import lax
from jax.experimental import pallas as pl
from jax.experimental.pallas import tpu as pltpu
from jax.sharding import Mesh, PartitionSpec as P

BLOCK = 128
GROUP = 8
STRIPES = 2
TILES_PER_STEP = 6

def invert_block(block):
    size = block.shape[0]
    lanes = lax.broadcasted_iota(jnp.int32, (1, size), 1)
    for j in range(0, size, GROUP):
        columns = [
            jnp.broadcast_to(block[:, j + k : j + k + 1], (size, size)) for k in range(GROUP)
        ]
        pivots = [
            [columns[b][j + a : j + a + 1, :] if b >= a else None for b in range(GROUP)]
            for a in range(GROUP)
        ]
        rows = []
        for a in range(GROUP):
            inside = (lanes >= j) & (lanes < j + GROUP)
            unit = jnp.where(lanes == j + a, 1.0, 0.0)
            rows.append(jnp.where(inside, unit, block[j + a : j + a + 1, :]))
        factors = [None] * GROUP
        for k in range(GROUP):
            scale = 1.0 / pivots[k][k]
            factors[k] = {}
            for a in range(k + 1, GROUP):
                factor = pivots[k][a] * scale
                factors[k][a] = factor
                rows[a] = rows[a] - factor * rows[k]
                for b in range(a, GROUP):
                    pivots[a][b] = pivots[a][b] - factor * pivots[k][b]
            pivots[k][k] = scale
        for k in reversed(range(GROUP)):
            solved = rows[k] * pivots[k][k]
            for a in range(k + 1, GROUP):
                solved = solved - factors[k][a] * rows[a]
            rows[k] = solved
        outside = (lanes < j) | (lanes >= j + GROUP)
        rest = jnp.where(outside, block, 0.0)
        for k in range(GROUP):
            rest = rest - columns[k] * rows[k]
        parts = []
        if j > 0:
            parts.append(rest[:j])
        parts.append(jnp.concatenate(rows, axis=0))
        if j + GROUP < size:
            parts.append(rest[j + GROUP :])
        block = jnp.concatenate(parts, axis=0)
    return block


def exact_dot(left, right):
    return jnp.dot(left, right, precision=lax.Precision.HIGHEST, preferred_element_type=jnp.float32)


def solve_kernel(diag_ref, panel_ref, out_ref, work_ref, rhs_ref):
    width = diag_ref.shape[0]
    tile = panel_ref.shape[0]
    work_ref[...] = diag_ref[...]
    rhs_ref[...] = panel_ref[...].astype(jnp.float32).T
    steps = width // BLOCK
    for k in range(steps):
        here = slice(k * BLOCK, (k + 1) * BLOCK)
        inverse = invert_block(work_ref[here, here])
        solved = exact_dot(inverse, rhs_ref[here, :])
        rhs_ref[here, :] = solved
        last = (k + 1) * BLOCK
        if last < width:
            rest = exact_dot(inverse, work_ref[here, last:])
            work_ref[here, last:] = rest
        for i in range(steps):
            if i == k:
                continue
            there = slice(i * BLOCK, (i + 1) * BLOCK)
            multiplier = work_ref[there, here]
            rhs_ref[there, :] = rhs_ref[there, :] - exact_dot(multiplier, solved)
            if last < width:
                work_ref[there, last:] = work_ref[there, last:] - exact_dot(multiplier, rest)
    solved = rhs_ref[...]
    high = solved.astype(jnp.bfloat16)
    low = (solved - high.astype(jnp.float32)).astype(jnp.bfloat16)
    out_ref[:, :tile] = high
    out_ref[:, tile:] = low


def solve_panel(diag, panel):
    width, tile = diag.shape[0], panel.shape[0]
    return pl.pallas_call(
        solve_kernel,
        out_shape=jax.ShapeDtypeStruct((width, 2 * tile), jnp.bfloat16),
        scratch_shapes=[
            pltpu.VMEM((width, width), jnp.float32),
            pltpu.VMEM((width, tile), jnp.float32),
        ],
        name="solve_panel",
    )(diag, panel)


def product_kernel(dest_ref, tiles_ref, solved_ref, sent_ref, kept_ref):
    slots, rows, width = sent_ref.shape
    tiles = tiles_ref.shape[0]
    step = pl.program_id(0)

    @pl.when(step == 0)
    def _():
        sent_ref[...] = jnp.zeros(sent_ref.shape, sent_ref.dtype)
        kept_ref[...] = jnp.zeros(kept_ref.shape, kept_ref.dtype)

    stacked = tiles_ref[...].reshape(tiles * rows, tiles_ref.shape[2])
    both = jnp.dot(stacked, solved_ref[...], preferred_element_type=jnp.float32)
    value = (both[:, :width] + both[:, width:]).astype(sent_ref.dtype)
    for t in range(tiles):
        dest = dest_ref[step * tiles + t]
        part = value[t * rows : (t + 1) * rows]

        @pl.when((dest >= 0) & (dest < slots))
        def _():
            sent_ref[dest] = part

        @pl.when(dest >= slots)
        def _():
            kept_ref[dest - slots] = part


def placed_products(dest, tiles, solved, slots, stripe, name):
    count, rows, width = tiles.shape
    rows = rows // STRIPES
    tile = solved.shape[1] // 2
    half = jax.ShapeDtypeStruct((slots, rows, tile), jnp.bfloat16)
    out = pl.BlockSpec((slots, rows, tile), lambda i, dest: (0, 0, 0))
    return pl.pallas_call(
        product_kernel,
        grid_spec=pltpu.PrefetchScalarGridSpec(
            num_scalar_prefetch=1,
            grid=(count // TILES_PER_STEP,),
            in_specs=[
                pl.BlockSpec((TILES_PER_STEP, rows, width), lambda i, dest: (i, stripe, 0)),
                pl.BlockSpec((width, 2 * tile), lambda i, dest: (0, 0)),
            ],
            out_specs=[out, out],
        ),
        out_shape=[half, half],
        name=name,
    )(dest, tiles, solved)


def local(diag_blocks, row_panel, col_panel, row_tiles, col_mask, slot_tile, trailing):
    width = row_panel.shape[2]
    count = row_tiles.shape[1]
    halves = lax.axis_size("x_hi")

    pair = lax.all_gather(row_panel[0], "x_hi", axis=0, tiled=True)
    tiles = lax.all_gather(pair, "z", axis=0, tiled=True).reshape(count, -1, width)
    solved = solve_panel(diag_blocks[0], col_panel[0])

    slots = slot_tile.shape[0] // 2
    ids = row_tiles[0].reshape(halves, count // halves).T.reshape(count)
    positions = jnp.arange(2 * slots, dtype=jnp.int32)
    match = slot_tile[None, :] == ids[:, None]
    kept_here = (positions % 2 == lax.axis_index("core")).astype(jnp.int32)
    target = jnp.where(col_mask[0, 0] != 0, positions // 2 + slots * kept_here, -1)
    dest = jnp.max(jnp.where(match, target[None, :], -1), axis=1)

    partials = []
    for stripe in range(STRIPES):
        sent, kept = placed_products(dest, tiles, solved, slots, stripe, f"products_{stripe}")
        received = lax.ppermute(sent, "core", [(0, 1), (1, 0)])
        partial = kept.astype(jnp.float32) + received.astype(jnp.float32)
        partials.append(partial.astype(jnp.bfloat16))
        if stripe == 0:
            dest, partials[0] = lax.optimization_barrier((dest, partials[0]))
    summed = lax.psum_scatter(
        partials[0].reshape(-1, partials[0].shape[2]), ("x_lo", "y"), scatter_dimension=0, tiled=True
    )
    pieces = lax.all_to_all(partials[1], ("x_lo", "y"), 0, 0, tiled=True)
    stripes = [summed.astype(jnp.float32), jnp.sum(pieces.astype(jnp.float32), axis=0)]
    return trailing - jnp.concatenate(stripes, axis=0)


def solution(mesh):
    wide, narrow = mesh.shape["wide"], mesh.shape["narrow"]
    split = Mesh(
        mesh.devices.reshape(2, wide // 4, 2, 2, narrow // 2), ("x_lo", "y", "core", "x_hi", "z")
    )
    w, n = ("x_lo", "y", "core"), ("x_hi", "z")
    placed = (P(w), P(w, n), P(w, n), P(w), P(w, n), P(), P(w, n))
    return jax.shard_map(local, mesh=split, in_specs=placed, out_specs=P(w, n), check_vma=False)
```
